32 devices in a mesh: ctx: 16 (over z, y, core), kvh: 2 (over x).
Axes of the slice: x: 2, y: 2, z: 4, core: 2. Of those that a mesh axis runs over, the one named last changes fastest.
Arguments:
- queries: bfloat16 [4096, 2048], P(('ctx', 'kvh')), may hold values from -6 to 6
- keys: bfloat16 [4096, 256], P(('ctx', 'kvh')), may hold values from -8 to 8
- values: bfloat16 [4096, 256], P(('ctx', 'kvh')), may hold values from -6 to 6
- grad_out: bfloat16 [4096, 2048], P(('ctx', 'kvh')), may hold values from -6 to 6
- doc_lengths: int32 [8], replicated, may hold values from 1 to 1024, 4096 in all
Outputs:
- attended: bfloat16 [4096, 2048], P(('ctx', 'kvh'))
- grad_queries: bfloat16 [4096, 2048], P(('ctx', 'kvh'))
- grad_keys: bfloat16 [4096, 256], P(('ctx', 'kvh'))
- grad_values: bfloat16 [4096, 256], P(('ctx', 'kvh'))
The draws below stay inside these ranges and needn't reach their ends.
Inputs may be any that keep to these rules, and one draw needn't show every extreme that they name: `doc_lengths`: 8 lengths that sum to 4096; the longest is exactly 1024.
All inputs are finite; a program needn't handle non-finite values.
Results may differ from the reference program's by a relative error of at most 0.0076.
Values may be sent and summed in bfloat16 or wider, within the bound.
A program may use at most 64 MiB of HBM per device.

```python
import math
import jax
import jax.numpy as jnp
import numpy as np
from jax import lax

HD = 128
QPG = 8
TD = 256
REACH = 4
KVH = 2
QH = 16
TOKENS = 4096
MAXDOC = 1024
DOCS = 8


def draw_queries(key, part):
    drawn = jax.random.normal(jax.random.fold_in(key, 1), (TOKENS, KVH, QPG, HD), jnp.float32)
    return jnp.clip(drawn, -6.0, 6.0).reshape(TOKENS, KVH * QPG * HD).astype(jnp.bfloat16)


def draw_keys(key, part):
    drawn = jax.random.normal(jax.random.fold_in(key, 2), (TOKENS, KVH, HD), jnp.float32)
    return jnp.clip(drawn, -8.0, 8.0).reshape(TOKENS, KVH * HD).astype(jnp.bfloat16)


def block_levels(key, shape, cuts, smallest, largest):
    factor_of = 1.0
    for axis_at, parts in cuts:
        heights = jax.random.uniform(jax.random.fold_in(jax.random.fold_in(key, 6), axis_at), (parts,), jnp.float32, smallest / len(cuts), largest / len(cuts))
        factor_of = factor_of * jnp.repeat(jnp.exp(heights), shape[axis_at] // parts).reshape((-1,) + (1,) * (len(shape) - 1 - axis_at))
    return factor_of


def profile(amount, total, bound, lean):
    portions = [(1 << 20) // math.isqrt(standing ** lean) + 1 for standing in range(2, amount + 1)]
    spare, given = total - bound - (amount - 1), [1] * (amount - 1)
    while spare > 0:
        free = [i for i in range(amount - 1) if given[i] < bound]
        pool, remaining = sum([portions[i] for i in free]), spare
        for i in free:
            extra = min(bound - given[i], max(1, remaining * portions[i] // pool), spare)
            given[i] = given[i] + extra
            spare = spare - extra
    return np.array([bound] + given)


def ragged_sizes(own_key, count, total, reach, skew):
    if count == 2:
        one = jax.random.randint(own_key, (), max(1, total - reach), min(reach, total - 1) + 1)
        return jnp.stack([one, total - one])
    sizes = jnp.asarray(profile(count, total, reach, skew), jnp.int32)
    couples = (count - 1) // 2
    giver, taker = sizes[1:1 + 2 * couples:2], sizes[2:2 + 2 * couples:2]
    margin = jnp.minimum(giver - 1, reach - taker)
    passed = jax.random.randint(jax.random.fold_in(own_key, 1), (couples,), 0, 1 << 20) % (margin + 1)
    sizes = sizes.at[1:1 + 2 * couples:2].set(giver - passed).at[2:2 + 2 * couples:2].set(taker + passed)
    return sizes[jax.random.permutation(jax.random.fold_in(own_key, 2), count)]


def gaussian(own_key, extent, spread, limit, shards=(), kind=jnp.bfloat16):
    entries = spread * jax.random.normal(own_key, extent, jnp.float32)
    if shards:
        entries = entries * block_levels(own_key, extent, shards, -0.22, 0.18)
    return jnp.clip(entries, -limit, limit).astype(kind)


def setup_inputs(seed: int = 0) -> dict:
    key_of = jax.random.split(jax.random.key(seed), 6)
    queries = draw_queries(jax.random.fold_in(key_of[5], 71), 0)
    keys = draw_keys(jax.random.fold_in(key_of[5], 71), 0)
    values = gaussian(key_of[2], (TOKENS, KVH * HD), 1.0, 6.0, ((0, 32),))
    grad_out = gaussian(key_of[3], (TOKENS, QH * HD), 1.0, 6.0, ((0, 32),))
    doc_lengths = ragged_sizes(key_of[4], DOCS, TOKENS, MAXDOC, 2).astype(jnp.int32)
    return {"queries": queries, "keys": keys, "values": values, "grad_out": grad_out, "doc_lengths": doc_lengths}


neg_large = -1e+30

def reference(queries, keys, values, grad_out, doc_lengths):
    lengths = doc_lengths.astype(jnp.int32)
    doc_ends = jnp.cumsum(lengths).astype(jnp.int32)
    starts = (doc_ends - lengths).astype(jnp.int32)
    scale_factor = 1.0 / math.sqrt(HD)
    offsets = jnp.arange(TD, dtype=jnp.int32)
    query_all = queries.reshape(TOKENS, KVH, QPG, HD)
    grad_all = grad_out.reshape(TOKENS, KVH, QPG, HD)
    zero_rows = jnp.zeros((MAXDOC, KVH, HD), jnp.bfloat16)
    key_all = jnp.concatenate([zero_rows, keys.reshape(TOKENS, KVH, HD)], 0)
    value_all = jnp.concatenate([zero_rows, values.reshape(TOKENS, KVH, HD)], 0)
    highest = lax.Precision.HIGHEST

    def first_of(positions):
        before_row = starts[None, :] <= positions[:, None]
        return lax.optimization_barrier(jnp.max(jnp.where(before_row, starts[None, :], 0), axis=1)).astype(jnp.int32)

    def block_inputs(block_index):
        first_row = (block_index * TD).astype(jnp.int32)
        query_block = lax.dynamic_slice_in_dim(query_all, first_row, TD, 0).astype(jnp.float32)
        grad_block = lax.dynamic_slice_in_dim(grad_all, first_row, TD, 0).astype(jnp.float32)
        query_pos = first_row + offsets
        return (first_row, query_block, grad_block, query_pos, first_of(query_pos))

    def tile_at(key_start, query_block, query_pos, doc_first):
        key_tile = lax.dynamic_slice_in_dim(key_all, key_start + MAXDOC, TD, 0).astype(jnp.float32)
        value_tile = lax.dynamic_slice_in_dim(value_all, key_start + MAXDOC, TD, 0).astype(jnp.float32)
        key_pos = key_start + offsets
        scores = jnp.einsum('qgpd,kgd->gpqk', query_block, key_tile, precision=highest) * scale_factor
        allowed = (key_pos[None, :] >= doc_first[:, None]) & (key_pos[None, :] <= query_pos[:, None])
        return (key_tile, value_tile, scores, allowed)

    def weights_of(scores, allowed, log_total):
        weights = jnp.where(allowed, jnp.exp(scores - log_total[..., None]), 0.0).astype(jnp.bfloat16)
        return lax.optimization_barrier(weights).astype(jnp.float32)

    def forward(block_index):
        first_row, query_block, grad_block, query_pos, doc_first = block_inputs(block_index)

        def gather_max(distance, loop_state):
            key_start = ((block_index - distance) * TD).astype(jnp.int32)

            def compute(partial_state):
                row_max, row_total = partial_state
                _, _, scores, allowed = tile_at(key_start, query_block, query_pos, doc_first)
                masked = jnp.where(allowed, scores, neg_large)
                new_max = jnp.maximum(row_max, masked.max(axis=3))
                row_total = row_total * jnp.exp(row_max - new_max) + lax.optimization_barrier(jnp.sum(jnp.where(allowed, jnp.exp(masked - new_max[..., None]), 0.0), axis=3))
                return (new_max, row_total)
            return lax.cond(doc_first[0] <= key_start + TD - 1, compute, lambda unchanged: unchanged, loop_state)
        start_state = (jnp.full((KVH, QPG, TD), neg_large, jnp.float32), jnp.zeros((KVH, QPG, TD), jnp.float32))
        row_max, row_total = lax.fori_loop(0, REACH + 1, gather_max, start_state)
        log_total = row_max + jnp.log(row_total)

        def add_out(distance, summed):
            key_start = ((block_index - distance) * TD).astype(jnp.int32)

            def compute(partial_state):
                _, value_tile, scores, allowed = tile_at(key_start, query_block, query_pos, doc_first)
                weights = weights_of(scores, allowed, log_total)
                return partial_state + jnp.einsum('gpqk,kgd->qgpd', weights, value_tile, precision=highest)
            return lax.cond(doc_first[0] <= key_start + TD - 1, compute, lambda unchanged: unchanged, summed)
        out_sum = lax.fori_loop(0, REACH + 1, add_out, jnp.zeros((TD, KVH, QPG, HD), jnp.float32))
        return (out_sum.astype(jnp.bfloat16), log_total)
    blocks = jnp.arange(TOKENS // TD, dtype=jnp.int32)
    attended_blocks, log_totals = lax.map(forward, blocks)
    attended = attended_blocks.reshape(TOKENS, QH * HD)
    kept_out = lax.optimization_barrier(attended)
    delta_all = lax.optimization_barrier(jnp.sum(grad_all.astype(jnp.float32) * kept_out.reshape(TOKENS, KVH, QPG, HD).astype(jnp.float32), axis=3))

    def backward(loop_state, inputs):
        block_index, log_total = inputs
        first_row, query_block, grad_block, query_pos, doc_first = block_inputs(block_index)
        delta_rows = jnp.transpose(lax.dynamic_slice_in_dim(delta_all, first_row, TD, 0), (1, 2, 0))

        def one_tile(distance, partial_state):
            key_start = ((block_index - distance) * TD).astype(jnp.int32)

            def compute(tile_state):
                grad_query, grad_key_sum, grad_value_sum = tile_state
                key_tile, value_tile, scores, allowed = tile_at(key_start, query_block, query_pos, doc_first)
                weights = weights_of(scores, allowed, log_total)
                grad_probs = jnp.einsum('qgpd,kgd->gpqk', grad_block, value_tile, precision=highest)
                grad_scores = (weights * (grad_probs - delta_rows[..., None]) * scale_factor).astype(jnp.bfloat16)
                grad_scores = lax.optimization_barrier(grad_scores).astype(jnp.float32)
                grad_query = grad_query + jnp.einsum('gpqk,kgd->qgpd', grad_scores, key_tile, precision=highest)
                key_part = jnp.einsum('gpqk,qgpd->kgd', grad_scores, query_block, precision=highest)
                value_part = jnp.einsum('gpqk,qgpd->kgd', weights, grad_block, precision=highest)
                row_at = key_start + MAXDOC
                grad_key_sum = lax.dynamic_update_slice_in_dim(grad_key_sum, lax.dynamic_slice_in_dim(grad_key_sum, row_at, TD, 0) + key_part, row_at, 0)
                grad_value_sum = lax.dynamic_update_slice_in_dim(grad_value_sum, lax.dynamic_slice_in_dim(grad_value_sum, row_at, TD, 0) + value_part, row_at, 0)
                return (grad_query, grad_key_sum, grad_value_sum)
            return lax.cond(doc_first[0] <= key_start + TD - 1, compute, lambda unchanged: unchanged, partial_state)
        start_query = jnp.zeros((TD, KVH, QPG, HD), jnp.float32)
        grad_query, grad_key_sum, grad_value_sum = lax.fori_loop(0, REACH + 1, one_tile, (start_query, loop_state[0], loop_state[1]))
        return ((grad_key_sum, grad_value_sum), grad_query.astype(jnp.bfloat16))
    zero_sums = jnp.zeros((TOKENS + MAXDOC, KVH, HD), jnp.float32)
    (grad_key_sum, grad_value_sum), grad_query_blocks = lax.scan(backward, (zero_sums, zero_sums), (blocks, log_totals))
    grad_queries = grad_query_blocks.reshape(TOKENS, QH * HD)
    grad_keys = grad_key_sum[MAXDOC:].astype(jnp.bfloat16).reshape(TOKENS, KVH * HD)
    grad_values = grad_value_sum[MAXDOC:].astype(jnp.bfloat16).reshape(TOKENS, KVH * HD)
    return (attended, grad_queries, grad_keys, grad_values)
```

```python
import functools
import math

import jax
import jax.numpy as jnp
from jax import lax
from jax.experimental import pallas as pl
from jax.experimental.pallas import tpu as pltpu
from jax.sharding import PartitionSpec as P

REACH = 4
LANES = 256
CORES = 2
SPAN = 384
NEG_LARGE = -1e30
F32 = jnp.float32
BF16 = jnp.bfloat16
MESH = pl.DeviceIdType.MESH
K, V = 0, 1


def matmul(a, b):
    return lax.dot_general(a, b, (((1,), (0,)), ((), ())), preferred_element_type=F32)


def both(*conditions):
    held = conditions[0]
    for condition in conditions[1:]:
        held = jnp.logical_and(held, condition)
    return held


def kernel(
    ranges, groups, head_width, doc_hbm, q_hbm, k_hbm, v_hbm, do_hbm,
    att_ref, gq_ref, gk_out, gv_out,
    q_ref, do_ref, kv_ref, kvt_ref, oth_ref, bias_ref, s_ref, e_ref, inv_ref, sdo_ref, sdot_ref,
    attb_ref, gqb_ref, out_ref, back_ref, prior_ref, own_ref, zsum_ref, zin_ref, fin_ref, doc_ref,
    load_sem, qload_sem, doc_sem, xq_send, xq_recv, own_send, z_send, fwd_send, kv_recv,
    back_send, back_recv, zs_send, zin_recv, xo_send, xo_recv, lo_sem,
):
    tokens = gk_out.shape[0]
    reach = REACH * groups
    share = groups // CORES
    slots = reach + groups + 1
    rows = REACH // CORES
    chips = rows * groups
    width = q_ref.shape[2]
    heads = width // head_width // share
    per_step = LANES // tokens
    steps = heads // per_step
    blocks = ranges * groups
    scale = 1.0 / math.sqrt(head_width)
    scale_2 = scale * math.log2(math.e)
    window = (reach + 1) * tokens

    ctx = lax.axis_index("ctx")
    column = lax.axis_index("kvh")
    me = ctx * groups + column
    place = me % reach
    band = me - place
    core = ctx % CORES
    row = place // (CORES * groups)
    low = row * CORES * groups + column
    partner = me + groups * (1 - 2 * core)
    has_prior = band > 0
    has_next = band + reach < blocks
    others = [(r, x) for r in range(rows) for x in range(groups) if (r, x) != (0, 0)]

    def device(block):
        return (block // groups, block % groups)

    def slot(k):
        if isinstance(k, int):
            return pl.ds(k * tokens, tokens)
        return pl.ds(pl.multiple_of(k * tokens, tokens), tokens)

    def columns_at(i, size):
        return pl.ds(pl.multiple_of(i * size, size), size)

    def chip(r, x):
        r_t = (row + r) % rows
        x_t = (column + x) % groups
        return r_t, x_t, r_t * CORES * groups + x_t

    def exists(k):
        return jnp.logical_or(has_prior, k >= reach - low)

    def send(src, dst, send_sem, recv_sem, block):
        return pltpu.make_async_remote_copy(
            src_ref=src, dst_ref=dst, send_sem=send_sem, recv_sem=recv_sem,
            device_id=device(block), device_id_type=MESH,
        )

    own_slot = reach + core * groups

    loads = {}
    for t, src in enumerate((k_hbm, v_hbm)):
        for j in range(share):
            loads[t, j] = [
                pltpu.make_async_copy(
                    src.at[:, columns_at(core * share + j, head_width)],
                    kv_ref.at[t, j, slot(own_slot), :], load_sem.at[t, j, 0],
                ),
                pltpu.make_async_copy(
                    src.at[:, columns_at((1 - core) * share + j, head_width)],
                    oth_ref.at[t, j], load_sem.at[t, j, 1],
                ),
            ]
            for copy in loads[t, j]:
                copy.start()
    doc_load = pltpu.make_async_copy(doc_hbm, doc_ref, doc_sem)
    doc_load.start()
    q_loads = [
        pltpu.make_async_copy(src.at[:, columns_at(core, width)], dst.at[core], qload_sem.at[i])
        for i, (src, dst) in enumerate(((q_hbm, q_ref), (do_hbm, do_ref)))
    ]
    for copy in q_loads:
        copy.start()
    q_passes = [
        send(src.at[:, columns_at(1 - core, width)], dst.at[core], xq_send.at[i], xq_recv.at[i], partner)
        for i, (src, dst) in enumerate(((q_hbm, q_ref), (do_hbm, do_ref)))
    ]
    q_arrivals = [
        send(src.at[:, columns_at(1 - core, width)], dst.at[1 - core], xq_send.at[i], xq_recv.at[i], partner)
        for i, (src, dst) in enumerate(((q_hbm, q_ref), (do_hbm, do_ref)))
    ]

    barrier = pltpu.get_barrier_semaphore()

    def greet(block):
        pl.semaphore_signal(barrier, 1, device_id=device(block), device_id_type=MESH)

    for d in range(1, reach):
        greet(band + (place + d) % reach)
    for near, step_to in ((has_next, reach), (has_prior, -reach)):

        @pl.when(near)
        def _():
            for c in range(CORES):
                greet(band + step_to + low + c * groups)

    pl.semaphore_wait(
        barrier,
        reach - 1 + jnp.where(has_next, CORES, 0) + jnp.where(has_prior, CORES, 0),
    )

    def kv_copy(t, j, far, send_sem, k, block):
        src = oth_ref.at[t, j] if far else kv_ref.at[t, j, slot(own_slot), :]
        return send(src, kv_ref.at[t, j, slot(k), :], send_sem, kv_recv.at[t, j, k], block)

    def z_copy(t, j, far):
        c = 1 - core if far else core
        return kv_copy(t, j, far, z_send.at[t, j, far], core * groups, band + reach + low + c * groups)

    def partner_copy(t, j):
        return kv_copy(t, j, 1, own_send.at[t, j, 0, 1], own_slot, partner)

    def own_copy(t, j, i, far):
        r_t, x_t, low_t = chip(*others[i])
        c = 1 - core if far else core
        return place < low_t + groups, kv_copy(
            t, j, far, own_send.at[t, j, i + 1, far], place - low_t + reach,
            band + low_t + c * groups,
        )

    def prior_copy(t, j, which, i):
        r_t, x_t, low_t = chip(*others[i])
        s = low + which * groups
        k = s - low_t
        return both(has_prior, low_t < s), send(
            kv_ref.at[t, j, slot(which * groups), :], kv_ref.at[t, j, slot(k), :],
            fwd_send.at[t, j, which, i], kv_recv.at[t, j, k], band + low_t + core * groups,
        )

    def arrival(t, j, k):
        return send(
            oth_ref.at[t, j], kv_ref.at[t, j, slot(k), :], z_send.at[t, j, 0], kv_recv.at[t, j, k], partner
        )

    def send_down(t):
        for j in range(share):
            for copy in loads[t, j]:
                copy.wait()

            @pl.when(has_next)
            def _():
                z_copy(t, j, 0).start()
                z_copy(t, j, 1).start()

            partner_copy(t, j).start()

    def send_own(t):
        for j in range(share):
            for i in range(len(others)):
                for far in range(CORES):
                    needed, copy = own_copy(t, j, i, far)

                    @pl.when(needed)
                    def _():
                        copy.start()

    def send_prior(t):
        for j in range(share):
            for which in range(CORES):

                @pl.when(has_prior)
                def _():
                    arrival(t, j, which * groups).wait_recv()

                for i in range(len(others)):
                    needed, copy = prior_copy(t, j, which, i)

                    @pl.when(needed)
                    def _():
                        copy.start()

    def receive(t):
        for j in range(share):
            for k in range(slots):
                if k in (0, groups):
                    continue
                needed = exists(k)
                if k in (reach, reach + groups):
                    needed = core != (k - reach) // groups

                @pl.when(needed)
                def _():
                    arrival(t, j, k).wait_recv()

    send_down(K)
    send_own(K)
    send_down(V)
    for copy in q_passes:
        copy.start()

    for k in range(reach):

        @pl.when(jnp.logical_not(exists(k)))
        def _():
            for t in (K, V):
                for j in range(share):
                    kv_ref[t, j, slot(k), :] = jnp.zeros((tokens, head_width), BF16)

    doc_load.wait()
    for blk in range(CORES):
        first_block = band + low + blk * groups
        query_pos = first_block * tokens + lax.broadcasted_iota(jnp.int32, (8, LANES), 1) % tokens

        def next_doc(i, carry):
            start, first = carry
            first = jnp.where(start <= query_pos, jnp.maximum(first, start), first)
            return start + doc_ref[i], first

        _, doc_first = lax.fori_loop(
            0, doc_ref.shape[0], next_doc, (jnp.int32(0), jnp.zeros((8, LANES), jnp.int32))
        )
        for s in range(reach + 1):
            key_pos = (first_block - reach + s) * tokens + lax.broadcasted_iota(jnp.int32, (tokens, LANES), 0)
            allowed = (key_pos >= doc_first[0:1]) & (key_pos <= query_pos[0:1])
            bias_ref[blk, slot(s), :] = jnp.where(allowed, 0.0, NEG_LARGE)

    send_prior(K)
    send_own(V)
    send_prior(V)
    for copy in q_loads:
        copy.wait()
    for copy in q_arrivals:
        copy.wait_recv()
    receive(K)

    units = [(j, blk, i) for j in range(share) for blk in range(CORES) for i in range(steps)]

    def head_columns(j, i, n):
        return pl.ds((j * heads + i * per_step + n) * head_width, head_width)

    def stacked(ref, j, blk, i):
        return jnp.concatenate(
            [ref[blk, :, head_columns(j, i, n)] for n in range(per_step)], axis=0
        )

    spans = [pl.ds(a, min(SPAN, window - a)) for a in range(0, window, SPAN)]

    def window_rows(blk, rows_in):
        return pl.ds(blk * groups * tokens + rows_in.start, rows_in.size)

    for u, (j, blk, i) in enumerate(units):
        s_buf = s_ref.at[u % 2]
        q_t = stacked(q_ref, j, blk, i).T
        top = jnp.full((8, LANES), NEG_LARGE, F32)
        for span in spans:
            scores = matmul(kv_ref[K, j, window_rows(blk, span), :], q_t) * scale_2 + bias_ref[blk, span, :]
            s_buf[span, :] = scores
            top = jnp.maximum(top, jnp.max(scores.reshape(-1, 8, LANES), axis=0))
        row_max = jnp.max(top, axis=0, keepdims=True)
        total = jnp.zeros((8, LANES), F32)
        for span in spans:
            weights = jnp.exp2(s_buf[span, :] - row_max)
            total = total + jnp.sum(weights.reshape(-1, 8, LANES), axis=0)
            e_ref[j, blk, span, i * LANES:(i + 1) * LANES] = weights.astype(BF16)
        inverse = 1.0 / jnp.sum(total, axis=0, keepdims=True)
        inv_ref[u] = inverse
        scaled_t = (stacked(do_ref, j, blk, i).T.astype(F32) * inverse).astype(BF16)
        sdot_ref[u] = scaled_t
        sdo_ref[j, blk, i * LANES:(i + 1) * LANES, :] = scaled_t.T

    pieces = []
    most = max(1, 4 * 128 // tokens)
    for first, last, blks in (
        (0, groups, (0,)), (groups, reach + 1, (0, 1)), (reach + 1, slots, (1,)),
    ):
        for a in range(first, last, most):
            pieces.append((a, min(a + most, last), blks))

    def back_copy(t, j, k):
        own = k >= reach - low
        s = jnp.where(own, k - reach + low, k + low)
        r_s = s // (CORES * groups)
        c_s = (s // groups) % CORES
        x_s = s % groups
        block = band + jnp.where(own, s, s + (core - c_s) * groups)
        i = ((row - r_s + rows) % rows) * groups + (column - x_s + groups) % groups
        entry = jnp.where(
            own, i * groups + core * share + j, chips * groups + (c_s * chips + i) * share + j
        )
        return send(
            out_ref.at[t, j, slot(k), :], back_ref.at[t, entry],
            back_send.at[t, j, k], back_recv.at[t, entry], block,
        )

    def back_needed(k):
        if k in (reach, reach + groups):
            return core != (k - reach) // groups
        return exists(k)

    def partials(t, left_ref, right, factor):
        for j in range(share):
            for first, last, blks in pieces:
                total = None
                for blk in blks:
                    part = pl.ds((first - blk * groups) * tokens, (last - first) * tokens)
                    term = matmul(left_ref[j, blk, part, :], right[j, blk])
                    total = term if total is None else total + term
                if factor is not None:
                    total = total * factor
                for k in range(first, last):
                    mine = total[(k - first) * tokens:(k - first + 1) * tokens]
                    if k in (0, groups):
                        prior_ref[t, j, k // groups] = mine
                        continue
                    if k in (reach, reach + groups):
                        own_ref[t, j, (k - reach) // groups] = mine
                    out_ref[t, j, slot(k), :] = mine.astype(BF16)
                for k in range(first, last):
                    if k in (0, groups):
                        continue

                    @pl.when(back_needed(k))
                    def _():
                        back_copy(t, j, k).start()

    def landed(t, entry):
        return send(
            oth_ref.at[t, 0], back_ref.at[t, entry], z_send.at[t, 0, 0], back_recv.at[t, entry], partner
        )

    def z_back(t, j, which):
        return send(
            zsum_ref.at[t, j, which], zin_ref.at[t, core * share + j],
            zs_send.at[t, j, which], zin_recv.at[t, core * share + j],
            band - reach + low + which * groups,
        )

    def collect_prior(t):
        for j in range(share):
            for which in range(CORES):
                for i in range(len(others)):
                    r_t, x_t, low_t = chip(*others[i])
                    entry = chips * groups + (which * chips + i + 1) * share + j

                    @pl.when(both(has_prior, low_t < low + which * groups))
                    def _():
                        landed(t, entry).wait_recv()
                        prior_ref[t, j, which] += back_ref[t, entry].astype(F32)

                @pl.when(has_prior)
                def _():
                    zsum_ref[t, j, which] = prior_ref[t, j, which].astype(BF16)
                    z_back(t, j, which).start()

    def collect_own(t, out):
        for c in range(CORES):

            @pl.when(core == c)
            def _():
                for j in range(share):
                    at = c * share + j
                    out[:, at * head_width:(at + 1) * head_width] = own_ref[t, j, c]
                    at = (1 - c) * share + j
                    landed(t, at).wait_recv()
                    out[:, at * head_width:(at + 1) * head_width] = back_ref[t, at].astype(F32)

        for i in range(len(others)):
            r_t, x_t, low_t = chip(*others[i])

            @pl.when(place < low_t + groups)
            def _():
                for g in range(groups):
                    entry = (i + 1) * groups + g
                    landed(t, entry).wait_recv()
                    out[:, g * head_width:(g + 1) * head_width] += back_ref[t, entry].astype(F32)

    def collect_next(t, out):
        @pl.when(has_next)
        def _():
            for g in range(groups):
                send(
                    oth_ref.at[t, 0], zin_ref.at[t, g], z_send.at[t, 0, 0], zin_recv.at[t, g], partner
                ).wait_recv()
                out[:, g * head_width:(g + 1) * head_width] += zin_ref[t, g].astype(F32)

    scaled = {(j, blk): sdo_ref[j, blk] for j in range(share) for blk in range(CORES)}
    partials(V, e_ref, scaled, None)

    receive(V)
    for j in range(share):
        for t in (K, V):
            for k in range(slots):
                kvt_ref[t, j, :, slot(k)] = kv_ref[t, j, slot(k), :].T

    for u, (j, blk, i) in enumerate(units):
        here = slice(i * LANES, (i + 1) * LANES)
        inverse = inv_ref[u]
        whole = pl.ds(blk * groups * tokens, window)
        out_t = (matmul(kvt_ref[V, j, :, whole], e_ref[j, blk, :, here]) * inverse).astype(BF16)
        do_t = stacked(do_ref, j, blk, i).T.astype(F32)
        delta = jnp.sum(out_t.astype(F32) * do_t, axis=0, keepdims=True) * inverse
        out = out_t.T
        scaled_t = sdot_ref[u]
        gq_t = jnp.zeros((head_width, LANES), F32)
        for span in spans:
            grad_probs = matmul(kv_ref[V, j, window_rows(blk, span), :], scaled_t)
            grad_scores = e_ref[j, blk, span, here] * (grad_probs - delta).astype(BF16)
            e_ref[j, blk, span, here] = grad_scores
            gq_t = gq_t + matmul(kvt_ref[K, j, :, window_rows(blk, span)], grad_scores)
        gq = (gq_t * scale).astype(BF16).T
        for n in range(per_step):
            attb_ref[blk, :, head_columns(j, i, n)] = out[n * tokens:(n + 1) * tokens]
            gqb_ref[blk, :, head_columns(j, i, n)] = gq[n * tokens:(n + 1) * tokens]
        if u == len(units) // 2 - 1:
            collect_prior(V)

    def exchange(i, buf, out):
        return (
            pltpu.make_async_copy(buf.at[core], out.at[:, columns_at(core, width)], lo_sem.at[i]),
            send(
                buf.at[1 - core], out.at[:, columns_at(core, width)], xo_send.at[i], xo_recv.at[i], partner
            ),
            send(
                buf.at[1 - core], out.at[:, columns_at(1 - core, width)], xo_send.at[i], xo_recv.at[i], partner
            ),
        )

    outs = [exchange(0, attb_ref, att_ref), exchange(1, gqb_ref, gq_ref)]
    for local, away, _ in outs:
        away.start()
        local.start()

    asked = {
        (j, blk): jnp.concatenate([stacked(q_ref, j, blk, i) for i in range(steps)], axis=0)
        for j in range(share) for blk in range(CORES)
    }
    partials(K, e_ref, asked, scale)

    for t in (V, K):
        if t == V:
            collect_prior(K)
        collect_own(t, fin_ref.at[t])
        collect_next(t, fin_ref.at[t])
    gv_out[...] = fin_ref[V].astype(BF16)
    gk_out[...] = fin_ref[K].astype(BF16)

    for local, away, coming in outs:
        local.wait()
        coming.wait_recv()
        away.wait_send()
    for copy in q_passes:
        copy.wait_send()
    for t in (K, V):
        for j in range(share):
            partner_copy(t, j).wait_send()

            @pl.when(has_next)
            def _():
                z_copy(t, j, 0).wait_send()
                z_copy(t, j, 1).wait_send()

            for i in range(len(others)):
                for far in range(CORES):
                    needed, copy = own_copy(t, j, i, far)

                    @pl.when(needed)
                    def _():
                        copy.wait_send()

                for which in range(CORES):
                    needed, copy = prior_copy(t, j, which, i)

                    @pl.when(needed)
                    def _():
                        copy.wait_send()

            for k in range(slots):
                if k in (0, groups):
                    continue

                @pl.when(back_needed(k))
                def _():
                    back_copy(t, j, k).wait_send()

            @pl.when(has_prior)
            def _():
                z_back(t, j, 0).wait_send()
                z_back(t, j, 1).wait_send()


def finish(a, b, c, d, out_a, out_b, out_c, out_d, sem):
    copies = [
        pltpu.make_async_copy(src, dst, sem.at[i])
        for i, (src, dst) in enumerate(((a, out_a), (b, out_b), (c, out_c), (d, out_d)))
    ]
    for copy in copies:
        copy.start()
    for copy in copies:
        copy.wait()


def on_device(ranges, groups, queries, keys, values, grad_out, doc_lengths):
    tokens = queries.shape[0]
    head_width = keys.shape[1] // groups
    share = groups // CORES
    reach = REACH * groups
    slots = reach + groups + 1
    window = (reach + 1) * tokens
    chips = REACH // CORES * groups
    width = queries.shape[1] // CORES
    per_step = LANES // tokens
    steps = queries.shape[1] // groups // head_width // per_step
    units = share * CORES * steps
    anywhere = pl.BlockSpec(memory_space=pl.ANY)
    vmem = pl.BlockSpec(memory_space=pltpu.VMEM)
    dma = pltpu.SemaphoreType.DMA
    shapes = [queries.shape, queries.shape, keys.shape, keys.shape]
    results = pl.pallas_call(
        functools.partial(kernel, ranges, groups, head_width),
        out_shape=tuple(jax.ShapeDtypeStruct(shape, BF16) for shape in shapes),
        in_specs=[anywhere] * 5,
        out_specs=[vmem] * 4,
        scratch_shapes=[
            pltpu.VMEM((CORES, tokens, width), BF16),
            pltpu.VMEM((CORES, tokens, width), BF16),
            pltpu.VMEM((2, share, slots * tokens, head_width), BF16),
            pltpu.VMEM((2, share, head_width, slots * tokens), BF16),
            pltpu.VMEM((2, share, tokens, head_width), BF16),
            pltpu.VMEM((CORES, window, LANES), F32),
            pltpu.VMEM((2, window, LANES), F32),
            pltpu.VMEM((share, CORES, window, steps * LANES), BF16),
            pltpu.VMEM((units, 1, LANES), F32),
            pltpu.VMEM((share, CORES, steps * LANES, head_width), BF16),
            pltpu.VMEM((units, head_width, LANES), BF16),
            pltpu.VMEM((CORES, tokens, width), BF16),
            pltpu.VMEM((CORES, tokens, width), BF16),
            pltpu.VMEM((2, share, slots * tokens, head_width), BF16),
            pltpu.VMEM((2, 2 * chips * groups, tokens, head_width), BF16),
            pltpu.VMEM((2, share, CORES, tokens, head_width), F32),
            pltpu.VMEM((2, share, CORES, tokens, head_width), F32),
            pltpu.VMEM((2, share, CORES, tokens, head_width), BF16),
            pltpu.VMEM((2, groups, tokens, head_width), BF16),
            pltpu.VMEM((2, tokens, groups * head_width), F32),
            pltpu.SMEM(doc_lengths.shape, jnp.int32),
            dma((2, share, 2)),
            dma((2,)),
            dma,
            dma((2,)),
            dma((2,)),
            dma((2, share, chips, CORES)),
            dma((2, share, CORES)),
            dma((2, share, CORES, chips)),
            dma((2, share, slots)),
            dma((2, share, slots)),
            dma((2, 2 * chips * groups)),
            dma((2, share, CORES)),
            dma((2, groups)),
            dma((2,)),
            dma((2,)),
            dma((2,)),
        ],
        compiler_params=pltpu.CompilerParams(
            collective_id=0, has_side_effects=True, vmem_limit_bytes=40 * 1024 * 1024
        ),
    )(*[
        pltpu.with_memory_space_constraint(x, pltpu.HBM)
        for x in (doc_lengths, queries, keys, values, grad_out)
    ])
    return pl.pallas_call(
        finish,
        out_shape=tuple(jax.ShapeDtypeStruct(shape, BF16) for shape in shapes),
        in_specs=[anywhere] * 4,
        out_specs=[anywhere] * 4,
        scratch_shapes=[dma((4,))],
        compiler_params=pltpu.CompilerParams(vmem_limit_bytes=4 * 1024 * 1024),
    )(*results)


def solution(mesh):
    rows = P(("ctx", "kvh"), None)
    return jax.shard_map(
        functools.partial(on_device, mesh.shape["ctx"], mesh.shape["kvh"]),
        mesh=mesh,
        in_specs=(rows, rows, rows, rows, P()),
        out_specs=(rows, rows, rows, rows),
        check_vma=False,
    )
```

```python
import functools
import math

import jax
import jax.numpy as jnp
from jax import lax
from jax.experimental import pallas as pl
from jax.experimental.pallas import tpu as pltpu
from jax.sharding import PartitionSpec as P

REACH = 4
LANES = 256
CORES = 2
SCORE_ROWS = 512
GRAD_ROWS = 256
AHEAD = 4
NEG_LARGE = -1e30
F32 = jnp.float32
BF16 = jnp.bfloat16
MESH = pl.DeviceIdType.MESH
K, V = 0, 1


def matmul(a, b):
    return lax.dot_general(a, b, (((1,), (0,)), ((), ())), preferred_element_type=F32)


def both(*conditions):
    held = conditions[0]
    for condition in conditions[1:]:
        held = jnp.logical_and(held, condition)
    return held


def kernel(
    ranges, groups, head_width, doc_hbm, q_hbm, k_hbm, v_hbm, do_hbm,
    att_ref, gq_ref, gk_out, gv_out,
    q_ref, do_ref, kv_ref, kvt_ref, oth_ref, bias_ref, s_ref, e_ref, d_ref, qt_ref, dot_ref, acc_ref, max_ref, sum_ref, fac_ref, delta_ref,
    sdo_ref, sdot_ref,
    attb_ref, gqb_ref, out_ref, back_ref, prior_ref, own_ref, zsum_ref, zin_ref, fin_ref, doc_ref,
    load_sem, qload_sem, doc_sem, xq_send, xq_recv, own_send, z_send, fwd_send, diag_send, band_sem, kv_recv,
    back_send, back_recv, zs_send, zin_recv, xo_send, xo_recv, lo_sem,
):
    tokens = gk_out.shape[0]
    reach = REACH * groups
    share = groups // CORES
    slots = reach + groups + 1
    rows = REACH // CORES
    chips = rows * groups
    width = q_ref.shape[2]
    heads = width // head_width // share
    per_step = LANES // tokens
    steps = heads // per_step
    blocks = ranges * groups
    scale = 1.0 / math.sqrt(head_width)
    scale_2 = scale * math.log2(math.e)

    ctx = lax.axis_index("ctx")
    column = lax.axis_index("kvh")
    me = ctx * groups + column
    place = me % reach
    band = me - place
    core = ctx % CORES
    row = place // (CORES * groups)
    low = row * CORES * groups + column
    partner = me + groups * (1 - 2 * core)
    has_prior = band > 0
    has_next = band + reach < blocks
    others = [(r, x) for r in range(rows) for x in range(groups) if (r, x) != (0, 0)]
    aligned = [i for i, (r, x) in enumerate(others) if r == 0 or x == 0]
    diagonal = [i for i in range(len(others)) if i not in aligned]

    def device(block):
        return (block // groups, block % groups)

    def slot(k):
        if isinstance(k, int):
            return pl.ds(k * tokens, tokens)
        return pl.ds(pl.multiple_of(k * tokens, tokens), tokens)

    def columns_at(i, size):
        return pl.ds(pl.multiple_of(i * size, size), size)

    def chip(r, x):
        r_t = (row + r) % rows
        x_t = (column + x) % groups
        return r_t, x_t, r_t * CORES * groups + x_t

    def exists(k):
        return jnp.logical_or(has_prior, k >= reach - low)

    def send(src, dst, send_sem, recv_sem, block):
        return pltpu.make_async_remote_copy(
            src_ref=src, dst_ref=dst, send_sem=send_sem, recv_sem=recv_sem,
            device_id=device(block), device_id_type=MESH,
        )

    own_slot = reach + core * groups

    loads = {}
    for t, src in enumerate((k_hbm, v_hbm)):
        for j in range(share):
            loads[t, j] = [
                pltpu.make_async_copy(
                    src.at[:, columns_at(core * share + j, head_width)],
                    kv_ref.at[t, j, slot(own_slot), :], load_sem.at[t, j, 0],
                ),
                pltpu.make_async_copy(
                    src.at[:, columns_at((1 - core) * share + j, head_width)],
                    oth_ref.at[t, j], load_sem.at[t, j, 1],
                ),
            ]
            for copy in loads[t, j]:
                copy.start()
    doc_load = pltpu.make_async_copy(doc_hbm, doc_ref, doc_sem)
    doc_load.start()
    q_loads = [
        pltpu.make_async_copy(src.at[:, columns_at(core, width)], dst.at[core], qload_sem.at[i])
        for i, (src, dst) in enumerate(((q_hbm, q_ref), (do_hbm, do_ref)))
    ]
    for copy in q_loads:
        copy.start()
    q_passes = [
        send(src.at[:, columns_at(1 - core, width)], dst.at[core], xq_send.at[i], xq_recv.at[i], partner)
        for i, (src, dst) in enumerate(((q_hbm, q_ref), (do_hbm, do_ref)))
    ]
    q_arrivals = [
        send(src.at[:, columns_at(1 - core, width)], dst.at[1 - core], xq_send.at[i], xq_recv.at[i], partner)
        for i, (src, dst) in enumerate(((q_hbm, q_ref), (do_hbm, do_ref)))
    ]

    barrier = pltpu.get_barrier_semaphore()

    def greet(block):
        pl.semaphore_signal(barrier, 1, device_id=device(block), device_id_type=MESH)

    for d in range(1, reach):
        greet(band + (place + d) % reach)
    for near, step_to in ((has_next, reach), (has_prior, -reach)):

        @pl.when(near)
        def _():
            for c in range(CORES):
                greet(band + step_to + low + c * groups)

    pl.semaphore_wait(
        barrier,
        reach - 1 + jnp.where(has_next, CORES, 0) + jnp.where(has_prior, CORES, 0),
    )

    @pl.when(has_prior)
    def _():
        pl.semaphore_signal(band_sem, 1, device_id=device(me - reach), device_id_type=MESH)

    def kv_copy(t, j, far, send_sem, k, block):
        src = oth_ref.at[t, j] if far else kv_ref.at[t, j, slot(own_slot), :]
        return send(src, kv_ref.at[t, j, slot(k), :], send_sem, kv_recv.at[t, j, k], block)

    def z_copy(t, j, far):
        c = 1 - core if far else core
        return kv_copy(t, j, far, z_send.at[t, j, far], core * groups, band + reach + low + c * groups)

    def partner_copy(t, j):
        return kv_copy(t, j, 1, own_send.at[t, j, 0, 1], own_slot, partner)

    def own_copy(t, j, i, far):
        r_t, x_t, low_t = chip(*others[i])
        c = 1 - core if far else core
        return place < low_t + groups, kv_copy(
            t, j, far, own_send.at[t, j, i + 1, far], place - low_t + reach,
            band + low_t + c * groups,
        )

    def diagonal_copy(t, j, i, far):
        r_t, x_t, low_t = chip(*others[i])
        c = 1 - core if far else core
        return both(has_next, low_t < place), kv_copy(
            t, j, far, diag_send.at[t, j, i, far], place - low_t, band + reach + low_t + c * groups
        )

    def prior_copy(t, j, which, i):
        r_t, x_t, low_t = chip(*others[i])
        s = low + which * groups
        k = s - low_t
        return both(has_prior, low_t < s), send(
            kv_ref.at[t, j, slot(which * groups), :], kv_ref.at[t, j, slot(k), :],
            fwd_send.at[t, j, which, i], kv_recv.at[t, j, k], band + low_t + core * groups,
        )

    def arrival(t, j, k):
        return send(
            oth_ref.at[t, j], kv_ref.at[t, j, slot(k), :], z_send.at[t, j, 0], kv_recv.at[t, j, k], partner
        )

    def send_down(t):
        for j in range(share):
            for copy in loads[t, j]:
                copy.wait()

            @pl.when(has_next)
            def _():
                z_copy(t, j, 0).start()
                z_copy(t, j, 1).start()

            partner_copy(t, j).start()

    def send_own(t):
        for j in range(share):
            for i in range(len(others)):
                for far in range(CORES):
                    needed, copy = own_copy(t, j, i, far)

                    @pl.when(needed)
                    def _():
                        copy.start()

    def send_prior(t):
        for j in range(share):
            for which in (core, 1 - core):

                @pl.when(has_prior)
                def _():
                    arrival(t, j, which * groups).wait_recv()

                for i in aligned:
                    needed, copy = prior_copy(t, j, which, i)

                    @pl.when(needed)
                    def _():
                        copy.start()

    def send_diagonal(t):
        for j in range(share):
            for i in diagonal:
                for far in range(CORES):
                    needed, copy = diagonal_copy(t, j, i, far)

                    @pl.when(needed)
                    def _():
                        copy.start()

    def receive(t, part):
        for j in range(share):
            for k in range(*part):
                if k in (0, groups):
                    continue
                needed = exists(k)
                if k in (reach, reach + groups):
                    needed = core != (k - reach) // groups

                @pl.when(needed)
                def _():
                    arrival(t, j, k).wait_recv()

    send_down(K)
    send_own(K)

    @pl.when(has_next)
    def _():
        pl.semaphore_wait(band_sem, 1)

    send_diagonal(K)
    send_down(V)
    send_diagonal(V)
    for copy in q_passes:
        copy.start()

    for k in range(reach):

        @pl.when(jnp.logical_not(exists(k)))
        def _():
            for t in (K, V):
                for j in range(share):
                    kv_ref[t, j, slot(k), :] = jnp.zeros((tokens, head_width), BF16)

    doc_load.wait()
    for blk in range(CORES):
        first_block = band + low + blk * groups
        query_pos = first_block * tokens + lax.broadcasted_iota(jnp.int32, (8, LANES), 1) % tokens

        def next_doc(i, carry):
            start, first = carry
            first = jnp.where(start <= query_pos, jnp.maximum(first, start), first)
            return start + doc_ref[i], first

        _, doc_first = lax.fori_loop(
            0, doc_ref.shape[0], next_doc, (jnp.int32(0), jnp.zeros((8, LANES), jnp.int32))
        )
        for s in range(reach + 1):
            key_pos = (first_block - reach + s) * tokens + lax.broadcasted_iota(jnp.int32, (tokens, LANES), 0)
            allowed = (key_pos >= doc_first[0:1]) & (key_pos <= query_pos[0:1])
            bias_ref[blk, slot(s), :] = jnp.where(allowed, 0.0, NEG_LARGE)

    send_prior(K)
    send_own(V)
    send_prior(V)
    for copy in q_loads:
        copy.wait()
    for copy in q_arrivals:
        copy.wait_recv()
    units = [(j, blk, i) for j in range(share) for blk in range(CORES) for i in range(steps)]
    near, far_half, near_half = (reach, slots), (0, reach // 2), (reach // 2, reach)
    parts = [near, far_half, near_half]

    def head_columns(j, i, n):
        return pl.ds((j * heads + i * per_step + n) * head_width, head_width)

    def stacked(ref, j, blk, i):
        return jnp.concatenate(
            [ref[blk, :, head_columns(j, i, n)] for n in range(per_step)], axis=0
        )

    def cut(blk, part):
        first = max(part[0], blk * groups)
        last = min(part[1], blk * groups + reach + 1)
        here = pl.ds(first * tokens, (last - first) * tokens)
        return here, pl.ds((first - blk * groups) * tokens, (last - first) * tokens)

    def chunks(rows_in, most):
        return [(a, min(most, rows_in.size - a)) for a in range(0, rows_in.size, most)]

    def lanes(i):
        return slice(i * LANES, (i + 1) * LANES)

    for r, part in enumerate(parts):
        receive(K, part)
        def scores_of(u):
            j, blk, i = units[u]
            s_buf = s_ref.at[u % 2]
            here, there = cut(blk, part)
            if r == 0:
                qt_ref[u] = stacked(q_ref, j, blk, i).T
            q_t = qt_ref[u]
            top = jnp.full((8, LANES), NEG_LARGE, F32)
            for a, n in chunks(here, SCORE_ROWS):
                scores = (
                    matmul(kv_ref[K, j, pl.ds(here.start + a, n), :], q_t) * scale_2
                    + bias_ref[blk, pl.ds(there.start + a, n), :]
                )
                s_buf[pl.ds(a, n), :] = scores
                top = jnp.maximum(top, jnp.max(scores.reshape(-1, 8, LANES), axis=0))
            return jnp.max(top, axis=0, keepdims=True)

        tops = [scores_of(0)]
        for u, (j, blk, i) in enumerate(units):
            s_buf = s_ref.at[u % 2]
            here, there = cut(blk, part)
            if u + 1 < len(units):
                tops.append(scores_of(u + 1))
            row_max = tops[u]
            total = jnp.zeros((8, LANES), F32)
            for a, n in chunks(here, SCORE_ROWS):
                weights = jnp.exp2(s_buf[pl.ds(a, n), :] - row_max)
                total = total + jnp.sum(weights.reshape(-1, 8, LANES), axis=0)
                e_ref[j, blk, pl.ds(there.start + a, n), lanes(i)] = weights.astype(BF16)
            max_ref[r, u] = row_max
            sum_ref[r, u] = jnp.sum(total, axis=0, keepdims=True)

    for u, (j, blk, i) in enumerate(units):
        row_max = jnp.maximum(jnp.maximum(max_ref[0, u], max_ref[1, u]), max_ref[2, u])
        shares = [jnp.exp2(max_ref[r, u] - row_max) for r in range(len(parts))]
        total = sum(shares[r] * sum_ref[r, u] for r in range(len(parts)))
        inverse = 1.0 / total
        do_t = stacked(do_ref, j, blk, i).T
        dot_ref[u] = do_t
        for r in range(len(parts)):
            factor = shares[r] * inverse
            fac_ref[r, u] = factor
            scaled_t = (do_t.astype(F32) * factor).astype(BF16)
            sdot_ref[r, u] = scaled_t
            sdo_ref[r, j, blk, lanes(i), :] = scaled_t.T

    most = max(1, 2 * 128 // tokens)

    def pieces(part):
        edges = [part[0]] + [k for k in (groups, reach + 1) if part[0] < k < part[1]] + [part[1]]
        for first, last in zip(edges[:-1], edges[1:]):
            blks = [blk for blk in range(CORES) if blk * groups <= first < blk * groups + reach + 1]
            for a in range(first, last, most):
                yield a, min(a + most, last), blks

    def back_copy(t, j, k):
        own = k >= reach - low
        s = jnp.where(own, k - reach + low, k + low)
        r_s = s // (CORES * groups)
        c_s = (s // groups) % CORES
        x_s = s % groups
        block = band + jnp.where(own, s, s + (core - c_s) * groups)
        i = ((row - r_s + rows) % rows) * groups + (column - x_s + groups) % groups
        entry = jnp.where(
            own, i * groups + core * share + j, chips * groups + (c_s * chips + i) * share + j
        )
        return send(
            out_ref.at[t, j, slot(k), :], back_ref.at[t, entry],
            back_send.at[t, j, k], back_recv.at[t, entry], block,
        )

    def back_needed(k):
        if k in (reach, reach + groups):
            return core != (k - reach) // groups
        return exists(k)

    def partials(t, part, left_ref, right, factor):
        for j in range(share):
            for first, last, blks in pieces(part):
                total = None
                for blk in blks:
                    there = pl.ds((first - blk * groups) * tokens, (last - first) * tokens)
                    term = matmul(left_ref[j, blk, there, :], right(j, blk))
                    total = term if total is None else total + term
                if factor is not None:
                    total = total * factor
                for k in range(first, last):
                    mine = total[(k - first) * tokens:(k - first + 1) * tokens]
                    if k in (0, groups):
                        prior_ref[t, j, k // groups] = mine
                        continue
                    if k in (reach, reach + groups):
                        own_ref[t, j, (k - reach) // groups] = mine
                    out_ref[t, j, slot(k), :] = mine.astype(BF16)

    def send_partials(t, part):
        for j in range(share):
            for k in range(*part):
                if k in (0, groups):
                    continue

                @pl.when(back_needed(k))
                def _():
                    back_copy(t, j, k).start()

    def landed(t, entry):
        return send(
            oth_ref.at[t, 0], back_ref.at[t, entry], z_send.at[t, 0, 0], back_recv.at[t, entry], partner
        )

    def z_back(t, j, which):
        return send(
            zsum_ref.at[t, j, which], zin_ref.at[t, core * share + j],
            zs_send.at[t, j, which], zin_recv.at[t, core * share + j],
            band - reach + low + which * groups,
        )

    def collect_prior(t):
        for j in range(share):
            for which in range(CORES):
                for i in range(len(others)):
                    r_t, x_t, low_t = chip(*others[i])
                    entry = chips * groups + (which * chips + i + 1) * share + j

                    @pl.when(both(has_prior, low_t < low + which * groups))
                    def _():
                        landed(t, entry).wait_recv()
                        prior_ref[t, j, which] += back_ref[t, entry].astype(F32)

                @pl.when(has_prior)
                def _():
                    zsum_ref[t, j, which] = prior_ref[t, j, which].astype(BF16)
                    z_back(t, j, which).start()

    def collect_own(t, out):
        for c in range(CORES):

            @pl.when(core == c)
            def _():
                for j in range(share):
                    at = c * share + j
                    out[:, at * head_width:(at + 1) * head_width] = own_ref[t, j, c]
                    at = (1 - c) * share + j
                    landed(t, at).wait_recv()
                    out[:, at * head_width:(at + 1) * head_width] = back_ref[t, at].astype(F32)

        for i in range(len(others)):
            r_t, x_t, low_t = chip(*others[i])

            @pl.when(place < low_t + groups)
            def _():
                for g in range(groups):
                    entry = (i + 1) * groups + g
                    landed(t, entry).wait_recv()
                    out[:, g * head_width:(g + 1) * head_width] += back_ref[t, entry].astype(F32)

    def collect_next(t, out):
        @pl.when(has_next)
        def _():
            for g in range(groups):
                send(
                    oth_ref.at[t, 0], zin_ref.at[t, g], z_send.at[t, 0, 0], zin_recv.at[t, g], partner
                ).wait_recv()
                out[:, g * head_width:(g + 1) * head_width] += zin_ref[t, g].astype(F32)

    def exchange(i, buf, out):
        return (
            pltpu.make_async_copy(buf.at[core], out.at[:, columns_at(core, width)], lo_sem.at[i]),
            send(
                buf.at[1 - core], out.at[:, columns_at(core, width)], xo_send.at[i], xo_recv.at[i], partner
            ),
            send(
                buf.at[1 - core], out.at[:, columns_at(1 - core, width)], xo_send.at[i], xo_recv.at[i], partner
            ),
        )

    outs = [exchange(0, attb_ref, att_ref), exchange(1, gqb_ref, gq_ref)]
    order = [1, 2, 0]

    def start_out(i):
        local, away, _ = outs[i]
        away.start()
        local.start()

    def value_gradients(r):
        partials(V, parts[r], e_ref, lambda j, blk: sdo_ref[r, j, blk], None)

    for r in order:
        value_gradients(r)
    for r in order:
        send_partials(V, parts[r])

    for r, part in enumerate(parts):
        receive(V, part)
        for j in range(share):
            for k in range(*part):
                kvt_ref[V, j, :, slot(k)] = kv_ref[V, j, slot(k), :].T
        def outputs_of(u):
            j, blk, i = units[u]
            here, there = cut(blk, part)
            return matmul(kvt_ref[V, j, :, here], e_ref[j, blk, there, lanes(i)])

        ahead = [outputs_of(u) for u in range(AHEAD)]
        for u, (j, blk, i) in enumerate(units):
            if u + AHEAD < len(units):
                ahead.append(outputs_of(u + AHEAD))
            term = ahead[u] * fac_ref[r, u]
            if r == 0:
                acc_ref[u] = term
            elif r < len(parts) - 1:
                acc_ref[u] += term
            else:
                out_t = (acc_ref[u] + term).astype(BF16)
                delta_ref[u] = jnp.sum(
                    out_t.astype(F32) * dot_ref[u].astype(F32), axis=0, keepdims=True
                )
                out = out_t.T
                for n in range(per_step):
                    attb_ref[blk, :, head_columns(j, i, n)] = out[n * tokens:(n + 1) * tokens]
    start_out(0)
    for j in range(share):
        for k in range(slots):
            kvt_ref[K, j, :, slot(k)] = kv_ref[K, j, slot(k), :].T

    def asked(j, blk):
        return jnp.concatenate([stacked(q_ref, j, blk, i) for i in range(steps)], axis=0)

    for at, r in enumerate(order):
        part = parts[r]
        items = []
        for u, (j, blk, i) in enumerate(units):
            here, there = cut(blk, part)
            for a, n in chunks(here, GRAD_ROWS):
                items.append((u, pl.ds(here.start + a, n), pl.ds(there.start + a, n), a == 0, a + n == here.size))

        def probs(item):
            u, mine, _, _, _ = item
            return matmul(kv_ref[V, units[u][0], mine, :], sdot_ref[r, u])

        ahead = [probs(item) for item in items[:AHEAD]]
        for at_item, (u, mine, window_at, starts, ends) in enumerate(items):
            j, blk, i = units[u]
            if at_item + AHEAD < len(items):
                ahead.append(probs(items[at_item + AHEAD]))
            grad_probs = ahead[at_item]
            ahead[at_item] = None
            if starts:
                delta = delta_ref[u] * fac_ref[r, u]
                gq_t = jnp.zeros((head_width, LANES), F32) if at == 0 else acc_ref[u]
            grad_scores = e_ref[j, blk, window_at, lanes(i)] * (grad_probs - delta).astype(BF16)
            d_ref[j, blk, window_at, lanes(i)] = grad_scores
            gq_t = gq_t + matmul(kvt_ref[K, j, :, mine], grad_scores)
            if not ends:
                continue
            if at < len(order) - 1:
                acc_ref[u] = gq_t
            else:
                gq = (gq_t * scale).astype(BF16).T
                for n in range(per_step):
                    gqb_ref[blk, :, head_columns(j, i, n)] = gq[n * tokens:(n + 1) * tokens]
        partials(K, part, d_ref, asked, scale)
        send_partials(K, part)
        if at == 1:
            collect_prior(V)
    start_out(1)

    collect_prior(K)

    for copy in q_passes:
        copy.wait_send()
    for t in (K, V):
        for j in range(share):
            partner_copy(t, j).wait_send()

            @pl.when(has_next)
            def _():
                z_copy(t, j, 0).wait_send()
                z_copy(t, j, 1).wait_send()

            for i in range(len(others)):
                for far in range(CORES):
                    needed, copy = own_copy(t, j, i, far)

                    @pl.when(needed)
                    def _():
                        copy.wait_send()

                if i in aligned:
                    waits = [prior_copy(t, j, which, i) for which in range(CORES)]
                else:
                    waits = [diagonal_copy(t, j, i, far) for far in range(CORES)]
                for needed, copy in waits:

                    @pl.when(needed)
                    def _():
                        copy.wait_send()

    for local, away, coming in outs:
        local.wait()
        coming.wait_recv()
        away.wait_send()
    for t in (V, K):
        collect_own(t, fin_ref.at[t])
    for t in (V, K):
        for j in range(share):
            for k in range(slots):
                if k in (0, groups):
                    continue

                @pl.when(back_needed(k))
                def _():
                    back_copy(t, j, k).wait_send()

    for t, result in ((V, gv_out), (K, gk_out)):
        collect_next(t, fin_ref.at[t])
        result[...] = fin_ref[t].astype(BF16)
        for j in range(share):

            @pl.when(has_prior)
            def _():
                z_back(t, j, 0).wait_send()
                z_back(t, j, 1).wait_send()


def finish(a, b, c, d, out_a, out_b, out_c, out_d, sem):
    copies = [
        pltpu.make_async_copy(src, dst, sem.at[i])
        for i, (src, dst) in enumerate(((a, out_a), (b, out_b), (c, out_c), (d, out_d)))
    ]
    for copy in copies:
        copy.start()
    for copy in copies:
        copy.wait()


def on_device(ranges, groups, queries, keys, values, grad_out, doc_lengths):
    tokens = queries.shape[0]
    head_width = keys.shape[1] // groups
    share = groups // CORES
    reach = REACH * groups
    slots = reach + groups + 1
    window = (reach + 1) * tokens
    chips = REACH // CORES * groups
    width = queries.shape[1] // CORES
    per_step = LANES // tokens
    steps = queries.shape[1] // groups // head_width // per_step
    units = share * CORES * steps
    anywhere = pl.BlockSpec(memory_space=pl.ANY)
    vmem = pl.BlockSpec(memory_space=pltpu.VMEM)
    dma = pltpu.SemaphoreType.DMA
    shapes = [queries.shape, queries.shape, keys.shape, keys.shape]
    results = pl.pallas_call(
        functools.partial(kernel, ranges, groups, head_width),
        out_shape=tuple(jax.ShapeDtypeStruct(shape, BF16) for shape in shapes),
        in_specs=[anywhere] * 5,
        out_specs=[vmem] * 4,
        scratch_shapes=[
            pltpu.VMEM((CORES, tokens, width), BF16),
            pltpu.VMEM((CORES, tokens, width), BF16),
            pltpu.VMEM((2, share, slots * tokens, head_width), BF16),
            pltpu.VMEM((2, share, head_width, slots * tokens), BF16),
            pltpu.VMEM((2, share, tokens, head_width), BF16),
            pltpu.VMEM((CORES, window, LANES), F32),
            pltpu.VMEM((2, reach // 2 * tokens, LANES), F32),
            pltpu.VMEM((share, CORES, window, steps * LANES), BF16),
            pltpu.VMEM((share, CORES, window, steps * LANES), BF16),
            pltpu.VMEM((units, head_width, LANES), BF16),
            pltpu.VMEM((units, head_width, LANES), BF16),
            pltpu.VMEM((units, head_width, LANES), F32),
            pltpu.VMEM((3, units, 1, LANES), F32),
            pltpu.VMEM((3, units, 1, LANES), F32),
            pltpu.VMEM((3, units, 1, LANES), F32),
            pltpu.VMEM((units, 1, LANES), F32),
            pltpu.VMEM((3, share, CORES, steps * LANES, head_width), BF16),
            pltpu.VMEM((3, units, head_width, LANES), BF16),
            pltpu.VMEM((CORES, tokens, width), BF16),
            pltpu.VMEM((CORES, tokens, width), BF16),
            pltpu.VMEM((2, share, slots * tokens, head_width), BF16),
            pltpu.VMEM((2, 2 * chips * groups, tokens, head_width), BF16),
            pltpu.VMEM((2, share, CORES, tokens, head_width), F32),
            pltpu.VMEM((2, share, CORES, tokens, head_width), F32),
            pltpu.VMEM((2, share, CORES, tokens, head_width), BF16),
            pltpu.VMEM((2, groups, tokens, head_width), BF16),
            pltpu.VMEM((2, tokens, groups * head_width), F32),
            pltpu.SMEM(doc_lengths.shape, jnp.int32),
            dma((2, share, 2)),
            dma((2,)),
            dma,
            dma((2,)),
            dma((2,)),
            dma((2, share, chips, CORES)),
            dma((2, share, CORES)),
            dma((2, share, CORES, chips)),
            dma((2, share, chips, CORES)),
            pltpu.SemaphoreType.REGULAR,
            dma((2, share, slots)),
            dma((2, share, slots)),
            dma((2, 2 * chips * groups)),
            dma((2, share, CORES)),
            dma((2, groups)),
            dma((2,)),
            dma((2,)),
            dma((2,)),
        ],
        compiler_params=pltpu.CompilerParams(
            collective_id=0, has_side_effects=True, vmem_limit_bytes=40 * 1024 * 1024
        ),
    )(*[
        pltpu.with_memory_space_constraint(x, pltpu.HBM)
        for x in (doc_lengths, queries, keys, values, grad_out)
    ])
    return pl.pallas_call(
        finish,
        out_shape=tuple(jax.ShapeDtypeStruct(shape, BF16) for shape in shapes),
        in_specs=[anywhere] * 4,
        out_specs=[anywhere] * 4,
        scratch_shapes=[dma((4,))],
        compiler_params=pltpu.CompilerParams(vmem_limit_bytes=4 * 1024 * 1024),
    )(*results)


def solution(mesh):
    rows = P(("ctx", "kvh"), None)
    return jax.shard_map(
        functools.partial(on_device, mesh.shape["ctx"], mesh.shape["kvh"]),
        mesh=mesh,
        in_specs=(rows, rows, rows, rows, P()),
        out_specs=(rows, rows, rows, rows),
        check_vma=False,
    )
```
